32 devices in a mesh: dp: 4 (over y, x), seq: 4 (over z), expert: 2 (over core).
Axes of the slice: x: 2, y: 2, z: 4, core: 2. Of those that a mesh axis runs over, the one named last changes fastest.
Arguments:
- queries: bfloat16 [8, 512, 2048], P(('dp', 'expert'), 'seq'), may hold values from -135 to 135
- keys: bfloat16 [8, 512, 2048], P(('dp', 'expert'), 'seq'), may hold values from -5 to 5
- values: bfloat16 [8, 512, 2048], P(('dp', 'expert'), 'seq'), may hold values from -6 to 6
- resid: bfloat16 [8, 512, 2048], P(('dp', 'expert'), 'seq'), may hold values from -20 to 20
- cotangent: bfloat16 [8, 512, 2048], P(('dp', 'expert'), 'seq'), may hold values from -0.3125 to 0.3125
- zone_ids: int32 [8, 512, 1], P(('dp', 'expert'), 'seq'), may hold values from 0 to 7; in each aligned block of 128 rows (0 to 127, 128 to 255, ..., all dimensions but the last counted through in order) at most 34 rows name the same one
- norm_gain: float32 [2048], replicated, may hold values from 0.1 to 1.9
- w_in: bfloat16 [8, 2048, 4096], P(('seq', 'expert'), None, 'dp'), may hold values from -0.125 to 0.125
- w_out: bfloat16 [8, 4096, 2048], P(('seq', 'expert'), 'dp'), may hold values from -0.09375 to 0.09375
Outputs:
- layer_out: bfloat16 [8, 512, 2048], P(('dp', 'expert'), 'seq')
- grad_w_in: bfloat16 [8, 2048, 4096], P(('seq', 'expert'), None, 'dp')
- grad_w_out: bfloat16 [8, 4096, 2048], P(('seq', 'expert'), 'dp')
The draws below stay inside these ranges and needn't reach their ends.
Inputs may be any that keep to these rules, and one draw needn't show every extreme that they name: `zone_ids`: among the tokens of one device at most 34 name the same expert, and that count is reached.
All inputs are finite; a program needn't handle non-finite values.
Results may differ from the reference program's by a relative error of at most 0.0085.
Values may be sent and summed in bfloat16 or wider, within the bound.
A program may use at most 128 MiB of HBM per device.

```python
import math
import jax
import jax.numpy as jnp
import numpy as np
from jax import lax

D = 2048
HEADS = 16
H = 4096
WIN_LEN = 512
HEAD_DIM = 128
SHARD_LEN = 128
WINDOWS = 8
TOKENS = 4096
EXPERTS = 8
CAP = 34
SLOTS = 1088


def common_plan(key):
    base_keys = jnp.clip(jax.random.normal(jax.random.fold_in(key, 101), (WINDOWS, WIN_LEN, D), jnp.float32), -5.0, 5.0)
    return base_keys


def draw_keys(key, part):
    base_keys = common_plan(key)
    return base_keys.astype(jnp.bfloat16)


def draw_queries(key, part):
    result = jnp.clip(jax.random.normal(jax.random.fold_in(key, 201), (WINDOWS, WIN_LEN, D), jnp.float32), -5.0, 5.0)
    return result.astype(jnp.bfloat16)


def draw_resid(key, part):
    extent = (WINDOWS, WIN_LEN, D)
    row_scale = jnp.exp(jax.random.uniform(jax.random.fold_in(key, 302), (WINDOWS, WIN_LEN, 1), jnp.float32, math.log(0.2), math.log(2.0)))
    col_scale = jnp.exp(jax.random.uniform(jax.random.fold_in(key, 303), (1, 1, D), jnp.float32, math.log(0.2), math.log(2.0)))
    jitter = jnp.clip(jax.random.normal(jax.random.fold_in(key, 301), extent, jnp.float32), -5.0, 5.0)
    return (jitter * row_scale * col_scale).astype(jnp.bfloat16)


def block_levels(key, shape, split, low, largest):
    level, own = 1.0, jax.random.fold_in(key, 6)
    for axis_at, blocks in split:
        steps = jnp.exp(jax.random.uniform(jax.random.fold_in(own, axis_at), (blocks,), jnp.float32, low / len(split), largest / len(split)))
        level = level * jnp.repeat(steps, shape[axis_at] // blocks).reshape([-1 if axis == axis_at else 1 for axis in range(len(shape))])
    return level


def routed_block(stream_key, own, number, rows, number_of, top, limit, lean):
    order = jax.random.permutation(stream_key, number_of)
    heavy_load, ordinary = shares(number_of, rows * top, limit, lean, True), shares(number_of, rows * top, limit, lean, False)
    places = jnp.arange(number_of)

    def named(lengths, offset_by):
        used = int((lengths > 0).sum())
        fixed = max(1, used // 4)
        passed = fixed + (places - fixed + offset_by * (used - fixed)) % max(1, number_of - fixed)
        return jnp.zeros((number_of,), jnp.int32).at[order[jnp.where(places < fixed, places, passed)]].set(jnp.asarray(lengths, jnp.int32))

    lengths = jnp.where(number % 4 == 0, named(heavy_load, number // 4), named(ordinary, number - number // 4 - 1))
    mixed = jax.random.permutation(jax.random.fold_in(own, 3), number_of)
    source_of, taker = mixed[0:number_of // 2 * 2:2], mixed[1:number_of // 2 * 2:2]
    slack = jnp.minimum(lengths[source_of] - 1, limit - lengths[taker]) // 2
    slack = jnp.where((source_of == order[0]) | (taker == order[0]) | (lengths[taker] == 0), 0, jnp.maximum(slack, 0))
    passed = jax.random.randint(jax.random.fold_in(own, 4), (number_of // 2,), 0, 1 << 20) % (slack + 1)
    lengths = lengths.at[source_of].add(-passed).at[taker].add(passed)
    labels = jnp.searchsorted(jnp.cumsum(lengths), jnp.arange(rows * top), side="right").astype(jnp.int32)
    table = labels.reshape(top, rows).T
    table = table[jax.random.permutation(jax.random.fold_in(own, 1), rows)]
    offset_by = jax.random.randint(jax.random.fold_in(own, 2), (rows, 1), 0, top)
    return jnp.take_along_axis(table, (jnp.arange(top)[None, :] + offset_by) % top, axis=1)


def shares(count, total, reach, lean, full):
    loads = [(1 << 20) // math.isqrt(standing ** lean) + 1 for standing in range(1, count + 1)]
    largest = reach if full else min(reach, max(-(-total // count), total * loads[0] // sum(loads)))
    least = 1 if total - largest >= count - 1 else 0
    holding, spare = [largest] + [least] * (count - 1), total - largest - least * (count - 1)
    while spare > 0:
        candidates = [i for i in range(1, count) if holding[i] < largest] or [i for i in range(1, count) if holding[i] < reach]
        whole, left = sum([loads[i] for i in candidates]), spare
        for i in candidates:
            addition = min(reach - holding[i], max(1, left * loads[i] // whole), spare)
            holding[i] = holding[i] + addition
            spare = spare - addition
    return np.array(holding)


def gaussian(rng, shape, width, reach, split=(), kind=jnp.bfloat16):
    values = jax.random.normal(rng, shape, jnp.float32) * width
    if len(split) > 0:
        values = block_levels(rng, shape, split, -0.22, 0.18) * values
    return jnp.clip(values, min=-reach, max=reach).astype(kind)


def setup_inputs(seed: int = 0) -> dict:
    seeds = jax.random.split(jax.random.key(seed), 10)
    queries = draw_queries(jax.random.fold_in(seeds[9], 71), 0)
    keys = draw_keys(jax.random.fold_in(seeds[9], 71), 0)
    values = gaussian(seeds[2], (WINDOWS, WIN_LEN, D), 1.0, 6.0, ((0, 8), (1, 4)))
    resid = draw_resid(jax.random.fold_in(seeds[9], 71), 0)
    cotangent = gaussian(seeds[4], (WINDOWS, WIN_LEN, D), 0.05, 0.3125, ((0, 8), (1, 4)))
    zone_ids_keys = jax.random.split(jax.random.fold_in(seeds[5], 1), WINDOWS * WIN_LEN // SHARD_LEN)
    zone_ids_turns = jax.random.permutation(jax.random.fold_in(seeds[5], 3), WINDOWS * WIN_LEN // SHARD_LEN)
    zone_ids = jax.vmap(lambda own, number: routed_block(jax.random.fold_in(seeds[5], 2), own, number, SHARD_LEN, EXPERTS, 1, CAP, 2))(zone_ids_keys, zone_ids_turns).reshape((WINDOWS, WIN_LEN, 1))
    norm_gain = jnp.clip(1.0 + 0.18 * jax.random.normal(seeds[6], (D,), jnp.float32), 0.1, 1.9)
    w_in = gaussian(seeds[7], (EXPERTS, D, H), D ** -0.5, 0.125, ((0, 8), (2, 4)))
    w_out = gaussian(seeds[8], (EXPERTS, H, D), H ** -0.5, 0.09375, ((0, 8), (1, 4)))
    return {"queries": queries, "keys": keys, "values": values, "resid": resid, "cotangent": cotangent, "zone_ids": zone_ids, "norm_gain": norm_gain, "w_in": w_in, "w_out": w_out}


epsilon = 1e-05

def attend(query_win, key_win, value_win):
    length = query_win.shape[0]
    q_heads = query_win.astype(jnp.float32).reshape(length, HEADS, HEAD_DIM)
    k_heads = key_win.astype(jnp.float32).reshape(length, HEADS, HEAD_DIM)
    v_heads = value_win.astype(jnp.float32).reshape(length, HEADS, HEAD_DIM)
    scores = jnp.einsum('shd,thd->hst', q_heads, k_heads) * (1.0 / math.sqrt(HEAD_DIM))
    peak = lax.optimization_barrier(jnp.max(scores, axis=-1, keepdims=True))
    weights = jnp.exp(scores - peak)
    totals = lax.optimization_barrier(jnp.sum(weights, axis=-1))
    rounded = lax.optimization_barrier(weights.astype(jnp.bfloat16)).astype(jnp.float32)
    head_out = jnp.einsum('hst,thd->hsd', rounded, v_heads) / totals[..., None]
    return head_out.transpose(1, 0, 2).reshape(length, HEADS * HEAD_DIM)

def reference(queries, keys, values, resid, cotangent, zone_ids, norm_gain, w_in, w_out):
    attended = lax.map(lambda triple: attend(triple[0], triple[1], triple[2]), (queries, keys, values))
    mixed = resid.astype(jnp.float32) + attended
    mean_sq = lax.optimization_barrier(jnp.mean(mixed * mixed, axis=-1, keepdims=True))
    normed = (mixed * lax.rsqrt(mean_sq + epsilon) * norm_gain.astype(jnp.float32)).astype(jnp.bfloat16)
    flat_x = jnp.concatenate([normed.reshape(TOKENS, D), jnp.zeros((1, D), jnp.bfloat16)], 0)
    flat_g = jnp.concatenate([cotangent.reshape(TOKENS, D), jnp.zeros((1, D), jnp.bfloat16)], 0)
    zone_flat = zone_ids.reshape(TOKENS)

    def one_expert(expert):
        chosen = jnp.nonzero(zone_flat == expert, size=SLOTS, fill_value=TOKENS)[0]
        inputs = flat_x[chosen]
        grads_in = flat_g[chosen]
        pre_act = jnp.dot(inputs, w_in[expert], preferred_element_type=jnp.float32)
        activated, pull_back = jax.vjp(jax.nn.gelu, pre_act)
        hidden = activated.astype(jnp.bfloat16)
        expert_out = jnp.dot(hidden, w_out[expert], preferred_element_type=jnp.float32).astype(jnp.bfloat16)
        back_proj = jnp.dot(grads_in, w_out[expert].T, preferred_element_type=jnp.float32)
        d_pre = pull_back(back_proj)[0].astype(jnp.bfloat16)
        grad_first = jnp.dot(inputs.T, d_pre, preferred_element_type=jnp.float32).astype(jnp.bfloat16)
        grad_second = jnp.dot(hidden.T, grads_in, preferred_element_type=jnp.float32).astype(jnp.bfloat16)
        return (chosen, expert_out, grad_first, grad_second)
    chosen_all, outs_all, grad_w_in, grad_w_out = lax.map(one_expert, jnp.arange(EXPERTS, dtype=jnp.int32))
    summed = jnp.zeros((TOKENS + 1, D), jnp.float32).at[chosen_all.reshape(-1)].add(outs_all.reshape(-1, D).astype(jnp.float32))
    layer_out = (mixed.reshape(TOKENS, D) + summed[:TOKENS]).astype(jnp.bfloat16)
    return (layer_out.reshape(WINDOWS, WIN_LEN, D), grad_w_in, grad_w_out)
```

```python
import functools
import math

import jax
import jax.numpy as jnp
from jax import lax
from jax.experimental import pallas as pl
from jax.experimental.pallas import tpu as pltpu
from jax.sharding import PartitionSpec as P

HEADS = 16
MESH = pl.DeviceIdType.MESH


epsilon = 1e-05


def remote(src, dst, send_sem, recv_sem, device):
    return pltpu.make_async_remote_copy(
        src_ref=src,
        dst_ref=dst,
        send_sem=send_sem,
        recv_sem=recv_sem,
        device_id=device,
        device_id_type=MESH,
    )


class Place:
    def __init__(self, sizes):
        self.groups, self.ring, self.pair = sizes
        self.owners = self.ring * self.pair
        self.dp = lax.axis_index("dp")
        self.seq = lax.axis_index("seq")
        self.me = self.seq * self.pair + lax.axis_index("expert")
        self.sides = (self.dp + 1 - 2 * (self.dp % 2), (self.dp + 2) % 4)

    def owner(self, index):
        return {"seq": index // self.pair, "expert": index % self.pair}

    def after(self, k):
        return (self.me + k) % self.owners

    def before(self, k):
        return (self.me + self.owners - k) % self.owners

    def greet(self):
        barrier = pltpu.get_barrier_semaphore()
        for k in range(1, self.owners):
            pl.semaphore_signal(
                barrier, inc=1, device_id=self.owner(self.after(k)), device_id_type=MESH
            )
        for side in self.sides:
            pl.semaphore_signal(barrier, inc=1, device_id={"dp": side}, device_id_type=MESH)
        pl.semaphore_wait(barrier, self.owners + 1)


class Dispatch:
    def __init__(self, place, send, out, sems):
        self.place, self.send, self.out = place, send, out
        self.z_send, self.z_recv, self.f_send, self.f_recv, self.r_send, self.r_recv, self.own = sems

    def slot(self, group, source):
        return self.out.at[group * self.place.owners + source]

    def along(self, k):
        p = self.place
        return remote(
            self.send.at[p.after(k)],
            self.slot(p.dp, p.me),
            self.z_send.at[k],
            self.z_recv.at[k],
            p.owner(p.after(k)),
        )

    def local(self):
        p = self.place
        return pltpu.make_async_copy(self.send.at[p.me], self.slot(p.dp, p.me), self.own)

    def forward(self, k, side):
        p = self.place
        src = self.send.at[p.me] if k == 0 else self.slot(p.dp, p.before(k))
        return remote(
            src,
            self.slot(p.dp, p.before(k)),
            self.f_send.at[k, side],
            self.f_recv.at[k, side],
            {"dp": p.sides[side]},
        )

    def relay(self, k):
        p = self.place
        come, go = k % 2, 1 - k % 2
        ref = self.slot(p.sides[come], p.before(k))
        return remote(ref, ref, self.r_send.at[k], self.r_recv.at[k], {"dp": p.sides[go]})

    def start(self):
        for k in range(1, self.place.owners):
            self.along(k).start()
        self.local().start()
        for side in range(2):
            self.forward(0, side).start()

    def pass_on(self, k):
        if k > 0:
            self.along(k).wait_recv()
            for side in range(2):
                self.forward(k, side).start()

    def pass_diagonal(self, k):
        self.forward(k, k % 2).wait_recv()
        self.relay(k).start()

    def finish(self):
        for k in range(self.place.owners):
            if k > 0:
                self.along(k).wait_send()
            self.forward(k, 0).wait_send()
            self.forward(k, 1).wait_send()
            self.forward(k, 1 - k % 2).wait_recv()
            self.relay(k).wait()
        self.local().wait()


def dispatch_sems(owners):
    dma = pltpu.SemaphoreType.DMA
    return [
        dma((owners,)),
        dma((owners,)),
        dma((owners, 2)),
        dma((owners, 2)),
        dma((owners,)),
        dma((owners,)),
        dma,
    ]


def attend_kernel(sizes, q, k, v, resid, gain, send_g, mixed, normed, arrived_g,
                  held, out, back, in_send, in_recv, own_sem, o_send, o_recv, *sems):
    place = Place(sizes)
    ring = place.ring
    heads, rows, width = held.shape[1], held.shape[3], held.shape[4]
    scale = 1.0 / math.sqrt(width)
    seq = place.seq

    def peer(j):
        return (seq + j) % ring

    def piece(kind, h, j):
        column = pl.multiple_of((peer(j) * heads + h) * width, width)
        return remote(
            (q, k, v)[kind].at[:, pl.ds(column, width)],
            held.at[kind, h, seq],
            in_send.at[kind, h, j - 1],
            in_recv.at[kind, h, j - 1],
            {"seq": peer(j)},
        )

    def own_piece(kind, h):
        column = pl.multiple_of((seq * heads + h) * width, width)
        return pltpu.make_async_copy(
            (q, k, v)[kind].at[:, pl.ds(column, width)], held.at[kind, h, seq], own_sem.at[kind, h]
        )

    def give_back(h, j):
        return remote(
            out.at[h, peer(j)],
            back.at[seq, h],
            o_send.at[h, j - 1],
            o_recv.at[h, j - 1],
            {"seq": peer(j)},
        )

    place.greet()
    tokens = Dispatch(place, send_g, arrived_g, sems)
    tokens.start()
    for h in range(heads):
        for kind in range(3):
            own_piece(kind, h).start()
            for j in range(1, ring):
                piece(kind, h, j).start()
    for n in range(place.owners):
        tokens.pass_on(n)
    relays = list(range(place.owners))
    for h in range(heads):
        for kind in range(3):
            own_piece(kind, h).wait()
            for j in range(1, ring):
                piece(kind, h, j).wait_recv()
        keys = held[1, h].reshape(ring * rows, width)
        vals = held[2, h].reshape(ring * rows, width)
        for j in range(ring):
            scores = (
                lax.dot_general(
                    held[0, h, j], keys, (((1,), (1,)), ((), ())), preferred_element_type=jnp.float32
                )
                * scale
            )
            weights = jnp.exp(scores - jnp.max(scores, axis=-1, keepdims=True))
            totals = jnp.sum(weights, axis=-1, keepdims=True)
            gained = jnp.dot(
                weights.astype(jnp.bfloat16), vals, preferred_element_type=jnp.float32
            )
            out[h, j] = (gained / totals).astype(jnp.bfloat16)
        for j in range(1, ring):
            give_back(h, j).start()
        back[seq, h] = out[h, seq]
        share = -(-place.owners // heads)
        for n in relays[h * share : (h + 1) * share]:
            tokens.pass_diagonal(n)
    for h in range(heads):
        for j in range(1, ring):
            give_back(h, j).wait_recv()
    step = 16

    @pl.loop(0, rows // step)
    def _(i):
        at = pl.ds(pl.multiple_of(i * step, step), step)
        total = jnp.zeros((step, 1), jnp.float32)
        for s in range(ring):
            for h in range(heads):
                cols = slice((s * heads + h) * width, (s * heads + h + 1) * width)
                value = resid[at, cols].astype(jnp.float32) + back[s, h, at, :].astype(jnp.float32)
                mixed[at, cols] = value
                total = total + jnp.sum(value * value, axis=-1, keepdims=True)
        factor = lax.rsqrt(total / resid.shape[1] + epsilon)
        normed[at, :] = (mixed[at, :] * factor * gain[...]).astype(jnp.bfloat16)

    for h in range(heads):
        for j in range(1, ring):
            give_back(h, j).wait_send()
            for kind in range(3):
                piece(kind, h, j).wait_send()
    tokens.finish()


def dispatch_kernel(sizes, send, arrived, *sems):
    place = Place(sizes)
    place.greet()
    tokens = Dispatch(place, send, arrived, sems)
    tokens.start()
    for n in range(place.owners):
        tokens.pass_on(n)
        if n > 0:
            tokens.pass_diagonal(n - 1)
    tokens.pass_diagonal(place.owners - 1)
    tokens.finish()


def combine_kernel(sizes, part, returned, first, mine, onward, second, a_send, a_recv, b_send,
                   b_recv, z_send, z_recv, own_sem):
    place = Place(sizes)
    owners = place.owners
    place.greet()

    def sides(k):
        return place.sides[k % 2], place.sides[1 - k % 2]

    def block(group, k):
        return part.at[group * owners + place.after(k)]

    def exchange(k, which):
        near, far = sides(k)
        other = (place.dp + 2) % 4 + 1 - 2 * (place.dp % 2)
        return remote(
            block(near if which == 0 else other, k),
            first.at[k, which],
            a_send.at[k, which],
            a_recv.at[k, which],
            {"dp": near},
        )

    def push(k):
        return remote(
            onward.at[k], second.at[k], b_send.at[k], b_recv.at[k], {"dp": sides(k)[1]}
        )

    def deliver(k):
        return remote(
            mine.at[k],
            returned.at[place.me],
            z_send.at[k],
            z_recv.at[k],
            place.owner(place.after(k)),
        )

    order = list(range(1, owners)) + [0]
    for k in order:
        exchange(k, 1).start()
        exchange(k, 0).start()

    def add(k):
        exchange(k, 1).wait_recv()
        far = sides(k)[1]
        onward[k] = (
            block(far, k)[...].astype(jnp.float32) + first[k, 1].astype(jnp.float32)
        ).astype(jnp.bfloat16)
        push(k).start()

    def close(k):
        exchange(k, 0).wait_recv()
        push(k).wait_recv()
        total = (
            block(place.dp, k)[...].astype(jnp.float32)
            + first[k, 0].astype(jnp.float32)
            + second[k].astype(jnp.float32)
        ).astype(jnp.bfloat16)
        mine[k] = total
        if k > 0:
            deliver(k).start()
        else:
            pltpu.make_async_copy(mine.at[0], returned.at[place.me], own_sem).start()

    lag = 2
    for n, k in enumerate(order):
        add(k)
        if n >= lag:
            close(order[n - lag])
    for k in order[owners - lag :]:
        close(k)
    for k in order:
        exchange(k, 0).wait_send()
        exchange(k, 1).wait_send()
        push(k).wait_send()
        if k > 0:
            deliver(k).wait()
    pltpu.make_async_copy(mine.at[0], returned.at[place.me], own_sem).wait()


def params(number):
    return pltpu.CompilerParams(
        collective_id=number, has_side_effects=True, vmem_limit_bytes=48 * 1024 * 1024
    )


ANY = pl.BlockSpec(memory_space=pl.ANY)
VMEM = pl.BlockSpec(memory_space=pltpu.VMEM)


def shards(sizes, queries, keys, values, resid, cotangent, zone_ids, norm_gain, w_in, w_out):
    rows = queries.shape[1]
    width = queries.shape[2]
    head_dim = width // HEADS
    groups, ring, pair = sizes
    owners = ring * pair
    heads = HEADS // ring
    capacity = 2 * rows // owners + 2
    padded = -(-capacity // 8) * 8
    dma = pltpu.SemaphoreType.DMA
    bf16, f32 = jnp.bfloat16, jnp.float32

    zone_of = zone_ids[0, :, 0]
    expert_hot = (zone_of[:, None] == jnp.arange(owners, dtype=jnp.int32)[None, :]).astype(
        jnp.int32
    )
    ranking = jnp.cumsum(expert_hot, axis=0) - 1
    slot_index = jnp.sum(ranking * expert_hot, axis=1)
    target = zone_of * padded + slot_index
    placing = (target[None, :] == jnp.arange(owners * padded, dtype=jnp.int32)[:, None]).astype(
        bf16
    )

    def placed(x):
        sent = jnp.dot(placing, x, preferred_element_type=f32).astype(bf16)
        return sent.reshape(owners, padded, width)

    slots = jax.ShapeDtypeStruct((groups * owners, padded, width), bf16)
    mixed, normed, arrived_g = pl.pallas_call(
        functools.partial(attend_kernel, sizes),
        out_shape=(
            jax.ShapeDtypeStruct((rows, width), f32),
            jax.ShapeDtypeStruct((rows, width), bf16),
            slots,
        ),
        in_specs=[ANY, ANY, ANY, VMEM, VMEM, VMEM],
        out_specs=(VMEM, VMEM, ANY),
        scratch_shapes=[
            pltpu.VMEM((3, heads, ring, rows, head_dim), bf16),
            pltpu.VMEM((heads, ring, rows, head_dim), bf16),
            pltpu.VMEM((ring, heads, rows, head_dim), bf16),
            dma((3, heads, ring - 1)),
            dma((3, heads, ring - 1)),
            dma((3, heads)),
            dma((heads, ring - 1)),
            dma((heads, ring - 1)),
            *dispatch_sems(owners),
        ],
        compiler_params=params(0),
        name="attend",
    )(queries[0], keys[0], values[0], resid[0], norm_gain[None, :], placed(cotangent[0]))

    arrived_x = pl.pallas_call(
        functools.partial(dispatch_kernel, sizes),
        out_shape=slots,
        in_specs=[VMEM],
        out_specs=ANY,
        scratch_shapes=dispatch_sems(owners),
        compiler_params=params(1),
        name="dispatch",
    )(placed(normed))

    slot_count = groups * owners * padded
    inputs = arrived_x.reshape(slot_count, width)
    grads_in = arrived_g.reshape(slot_count, width)
    w_first = w_in[0]
    w_second = w_out[0]
    pre_act = jnp.dot(inputs, w_first, preferred_element_type=f32)
    activated, pull_back = jax.vjp(jax.nn.gelu, pre_act)
    hidden = activated.astype(bf16)
    back_proj = lax.dot_general(
        grads_in, w_second, (((1,), (1,)), ((), ())), preferred_element_type=f32
    )
    d_pre = pull_back(back_proj)[0].astype(bf16)
    grad_first = lax.dot_general(
        inputs, d_pre, (((0,), (0,)), ((), ())), preferred_element_type=f32
    ).astype(bf16)
    grad_second = lax.dot_general(
        hidden, grads_in, (((0,), (0,)), ((), ())), preferred_element_type=f32
    ).astype(bf16)
    part = jnp.dot(hidden, w_second, preferred_element_type=f32).astype(bf16)

    returned = pl.pallas_call(
        functools.partial(combine_kernel, sizes),
        out_shape=jax.ShapeDtypeStruct((owners, padded, width), bf16),
        in_specs=[VMEM],
        out_specs=VMEM,
        scratch_shapes=[
            pltpu.VMEM((owners, 2, padded, width), bf16),
            pltpu.VMEM((owners, padded, width), bf16),
            pltpu.VMEM((owners, padded, width), bf16),
            pltpu.VMEM((owners, padded, width), bf16),
            dma((owners, 2)),
            dma((owners, 2)),
            dma((owners,)),
            dma((owners,)),
            dma((owners,)),
            dma((owners,)),
            dma,
        ],
        compiler_params=params(2),
        name="combine",
    )(part.reshape(groups * owners, padded, width))

    expert_rows = lax.dot_general(
        placing,
        returned.reshape(owners * padded, width),
        (((0,), (0,)), ((), ())),
        preferred_element_type=f32,
    )
    layer_out = (mixed + expert_rows).astype(bf16)[None]
    return (layer_out, grad_first[None], grad_second[None])


def solution(mesh):
    sizes = tuple(mesh.shape[name] for name in ("dp", "seq", "expert"))
    placed = (
        P(("dp", "expert"), "seq", None),
        P(("dp", "expert"), "seq", None),
        P(("dp", "expert"), "seq", None),
        P(("dp", "expert"), "seq", None),
        P(("dp", "expert"), "seq", None),
        P(("dp", "expert"), "seq", None),
        P(),
        P(("seq", "expert"), None, "dp"),
        P(("seq", "expert"), "dp", None),
    )
    return jax.shard_map(
        functools.partial(shards, sizes),
        mesh=mesh,
        in_specs=placed,
        out_specs=(
            P(("dp", "expert"), "seq", None),
            P(("seq", "expert"), None, "dp"),
            P(("seq", "expert"), "dp", None),
        ),
        check_vma=False,
    )
```

```python
import functools
import math

import jax
import jax.numpy as jnp
from jax import lax
from jax.experimental import pallas as pl
from jax.experimental.pallas import tpu as pltpu
from jax.sharding import PartitionSpec as P

HEADS = 16
MESH = pl.DeviceIdType.MESH


epsilon = 1e-05


def remote(src, dst, send_sem, recv_sem, device):
    return pltpu.make_async_remote_copy(
        src_ref=src,
        dst_ref=dst,
        send_sem=send_sem,
        recv_sem=recv_sem,
        device_id=device,
        device_id_type=MESH,
    )


class Place:
    def __init__(self, sizes):
        self.groups, self.ring, self.pair = sizes
        self.owners = self.ring * self.pair
        self.dp = lax.axis_index("dp")
        self.seq = lax.axis_index("seq")
        self.me = self.seq * self.pair + lax.axis_index("expert")
        self.sides = (self.dp + 1 - 2 * (self.dp % 2), (self.dp + 2) % 4)

    def owner(self, index):
        return {"seq": index // self.pair, "expert": index % self.pair}

    def after(self, k):
        return (self.me + k) % self.owners

    def before(self, k):
        return (self.me + self.owners - k) % self.owners

    def greet(self):
        barrier = pltpu.get_barrier_semaphore()
        for k in range(1, self.owners):
            pl.semaphore_signal(
                barrier, inc=1, device_id=self.owner(self.after(k)), device_id_type=MESH
            )
        for side in self.sides:
            pl.semaphore_signal(barrier, inc=1, device_id={"dp": side}, device_id_type=MESH)
        pl.semaphore_wait(barrier, self.owners + 1)


class Dispatch:
    def __init__(self, place, send, out, sems):
        self.place, self.send, self.out = place, send, out
        self.z_send, self.z_recv, self.f_send, self.f_recv, self.r_send, self.r_recv, self.own = sems

    def slot(self, group, source):
        index = group * self.place.owners + source
        if len(self.out.shape) == 3:
            return self.out.at[index]
        padded = self.send.shape[1]
        return self.out.at[pl.ds(pl.multiple_of(index * padded, 8), padded)]

    def along(self, k):
        p = self.place
        return remote(
            self.send.at[p.after(k)],
            self.slot(p.dp, p.me),
            self.z_send.at[k],
            self.z_recv.at[k],
            p.owner(p.after(k)),
        )

    def local(self):
        p = self.place
        return pltpu.make_async_copy(self.send.at[p.me], self.slot(p.dp, p.me), self.own)

    def forward(self, k, side):
        p = self.place
        src = self.send.at[p.me] if k == 0 else self.slot(p.dp, p.before(k))
        return remote(
            src,
            self.slot(p.dp, p.before(k)),
            self.f_send.at[k, side],
            self.f_recv.at[k, side],
            {"dp": p.sides[side]},
        )

    def relay(self, k):
        p = self.place
        come, go = k % 2, 1 - k % 2
        ref = self.slot(p.sides[come], p.before(k))
        return remote(ref, ref, self.r_send.at[k], self.r_recv.at[k], {"dp": p.sides[go]})

    def start(self):
        for k in range(1, self.place.owners):
            self.along(k).start()
        self.local().start()
        for side in range(2):
            self.forward(0, side).start()

    def pass_on(self, k):
        if k > 0:
            self.along(k).wait_recv()
            for side in range(2):
                self.forward(k, side).start()

    def pass_diagonal(self, k):
        self.forward(k, k % 2).wait_recv()
        self.relay(k).start()

    def rest_of_side(self, side):
        for k in range(self.place.owners):
            if k % 2 != side:
                self.forward(k, side).wait_recv()

    def corner(self):
        for k in range(self.place.owners):
            self.relay(k).wait_recv()

    def sent(self):
        for k in range(self.place.owners):
            if k > 0:
                self.along(k).wait_send()
            self.forward(k, 0).wait_send()
            self.forward(k, 1).wait_send()
            self.relay(k).wait_send()

    def finish(self):
        self.local().wait()
        self.rest_of_side(0)
        self.rest_of_side(1)
        self.corner()
        self.sent()


def dispatch_sems(owners):
    dma = pltpu.SemaphoreType.DMA
    return [
        dma((owners,)),
        dma((owners,)),
        dma((owners, 2)),
        dma((owners, 2)),
        dma((owners,)),
        dma((owners,)),
        dma,
    ]


def attend_kernel(sizes, q, k, v, resid, gain, send_g, mixed, normed, arrived_g,
                  held, out, back, in_send, in_recv, own_sem, o_send, o_recv, *sems):
    place = Place(sizes)
    ring = place.ring
    heads, rows, width = held.shape[1], held.shape[3], held.shape[4]
    scale = 1.0 / math.sqrt(width)
    seq = place.seq

    def peer(j):
        return (seq + j) % ring

    def piece(kind, h, j):
        column = pl.multiple_of((peer(j) * heads + h) * width, width)
        return remote(
            (q, k, v)[kind].at[:, pl.ds(column, width)],
            held.at[kind, h, seq],
            in_send.at[kind, h, j - 1],
            in_recv.at[kind, h, j - 1],
            {"seq": peer(j)},
        )

    def own_piece(kind, h):
        column = pl.multiple_of((seq * heads + h) * width, width)
        return pltpu.make_async_copy(
            (q, k, v)[kind].at[:, pl.ds(column, width)], held.at[kind, h, seq], own_sem.at[kind, h]
        )

    def give_back(h, j):
        return remote(
            out.at[h, peer(j)],
            back.at[seq, h],
            o_send.at[h, j - 1],
            o_recv.at[h, j - 1],
            {"seq": peer(j)},
        )

    place.greet()
    tokens = Dispatch(place, send_g, arrived_g, sems)
    tokens.start()
    for h in range(heads):
        for kind in range(3):
            own_piece(kind, h).start()
            for j in range(1, ring):
                piece(kind, h, j).start()
    for n in range(place.owners):
        tokens.pass_on(n)
    relays = list(range(place.owners))
    for h in range(heads):
        for kind in range(3):
            own_piece(kind, h).wait()
            for j in range(1, ring):
                piece(kind, h, j).wait_recv()
        keys = held[1, h].reshape(ring * rows, width)
        vals = held[2, h].reshape(ring * rows, width)
        for j in range(ring):
            scores = (
                lax.dot_general(
                    held[0, h, j], keys, (((1,), (1,)), ((), ())), preferred_element_type=jnp.float32
                )
                * scale
            )
            weights = jnp.exp(scores - jnp.max(scores, axis=-1, keepdims=True))
            totals = jnp.sum(weights, axis=-1, keepdims=True)
            gained = jnp.dot(
                weights.astype(jnp.bfloat16), vals, preferred_element_type=jnp.float32
            )
            out[h, j] = (gained / totals).astype(jnp.bfloat16)
        for j in range(1, ring):
            give_back(h, j).start()
        back[seq, h] = out[h, seq]
        share = -(-place.owners // heads)
        for n in relays[h * share : (h + 1) * share]:
            tokens.pass_diagonal(n)
    for h in range(heads):
        for j in range(1, ring):
            give_back(h, j).wait_recv()
    step = 16

    @pl.loop(0, rows // step)
    def _(i):
        at = pl.ds(pl.multiple_of(i * step, step), step)
        total = jnp.zeros((step, 1), jnp.float32)
        for s in range(ring):
            for h in range(heads):
                cols = slice((s * heads + h) * width, (s * heads + h + 1) * width)
                value = resid[at, cols].astype(jnp.float32) + back[s, h, at, :].astype(jnp.float32)
                mixed[at, cols] = value
                total = total + jnp.sum(value * value, axis=-1, keepdims=True)
        factor = lax.rsqrt(total / resid.shape[1] + epsilon)
        normed[at, :] = (mixed[at, :] * factor * gain[...]).astype(jnp.bfloat16)

    for h in range(heads):
        for j in range(1, ring):
            give_back(h, j).wait_send()
            for kind in range(3):
                piece(kind, h, j).wait_send()
    tokens.finish()


def gelu_and_slope(x):
    root = math.sqrt(2.0 / math.pi)
    square = x * x
    curve = jnp.tanh(root * (x + 0.044715 * (square * x)))
    half = 0.5 * (1.0 + curve)
    slope = half + 0.5 * x * (1.0 - curve * curve) * (root * (1.0 + 3 * 0.044715 * square))
    return x * half, slope


def dispatch_kernel(sizes, send, g, w_first, w_second, arrived, hidden, d_pre,
                    g_held, in_held, out_held, back_held, g_sem, in_sem, out_sem, *sems):
    place = Place(sizes)
    owners = place.owners
    loads = (
        pltpu.make_async_copy(w_second, out_held, out_sem),
        pltpu.make_async_copy(g, g_held, g_sem),
        pltpu.make_async_copy(w_first, in_held, in_sem),
    )
    for load in loads:
        load.start()
    place.greet()
    tokens = Dispatch(place, send, arrived, sems)
    tokens.start()
    pieces = 8
    size = g_held.shape[0] // pieces
    width = 256

    def project(n):
        back_held[n * size : (n + 1) * size, :] = lax.dot_general(
            g_held[n * size : (n + 1) * size, :],
            out_held[...],
            (((1,), (1,)), ((), ())),
            preferred_element_type=jnp.float32,
        )

    def expert(group):
        count = owners * send.shape[1]
        at = pl.ds(pl.multiple_of(group * count, 16), count)

        @pl.loop(0, in_held.shape[1] // width)
        def _(c):
            cols = pl.ds(pl.multiple_of(c * width, width), width)
            pre = jnp.dot(arrived[at, :], in_held[:, cols], preferred_element_type=jnp.float32)
            value, slope = gelu_and_slope(pre)
            hidden[at, cols] = value.astype(jnp.bfloat16)
            d_pre[at, cols] = (slope * back_held[at, cols]).astype(jnp.bfloat16)

    loads[0].wait()
    loads[1].wait()
    for n in range(owners):
        for piece in range(n * pieces // owners, (n + 1) * pieces // owners):
            project(piece)
        tokens.pass_on(n)
        if n > 0:
            tokens.pass_diagonal(n - 1)
    tokens.pass_diagonal(owners - 1)
    loads[2].wait()
    tokens.local().wait()
    expert(place.dp)
    for side in range(2):
        tokens.rest_of_side(side)
        expert(place.sides[side])
    tokens.corner()
    expert((place.sides[0] + 2) % 4)
    tokens.sent()


def combine_kernel(sizes, part, x, d_pre, hidden, g, returned, grad_first, grad_second, first,
                   mine, onward, second, x_held, d_held, h_held, g_held, a_send, a_recv, b_send,
                   b_recv, z_send, z_recv, load_sem, own_sem):
    place = Place(sizes)
    owners = place.owners
    loads = [
        pltpu.make_async_copy(src, dst, load_sem.at[n])
        for n, (src, dst) in enumerate(
            ((x, x_held), (d_pre, d_held), (hidden, h_held), (g, g_held))
        )
    ]
    for load in loads:
        load.start()
    place.greet()
    pieces = 8

    def gradients(n):
        for left, right, grad in ((x_held, d_held, grad_first), (h_held, g_held, grad_second)):
            size = left.shape[1] // pieces
            grad[n * size : (n + 1) * size, :] = lax.dot_general(
                left[:, n * size : (n + 1) * size],
                right[...],
                (((0,), (0,)), ((), ())),
                preferred_element_type=jnp.float32,
            ).astype(jnp.bfloat16)

    def sides(k):
        return place.sides[k % 2], place.sides[1 - k % 2]

    def block(group, k):
        return part.at[group * owners + place.after(k)]

    def exchange(k, which):
        near, far = sides(k)
        other = (place.dp + 2) % 4 + 1 - 2 * (place.dp % 2)
        return remote(
            block(near if which == 0 else other, k),
            first.at[k, which],
            a_send.at[k, which],
            a_recv.at[k, which],
            {"dp": near},
        )

    def push(k):
        return remote(
            onward.at[k], second.at[k], b_send.at[k], b_recv.at[k], {"dp": sides(k)[1]}
        )

    def deliver(k):
        return remote(
            mine.at[k],
            returned.at[place.me],
            z_send.at[k],
            z_recv.at[k],
            place.owner(place.after(k)),
        )

    order = list(range(1, owners)) + [0]
    ahead = min(4, owners)

    def open_exchange(k):
        exchange(k, 1).start()
        exchange(k, 0).start()

    for k in order[:ahead]:
        open_exchange(k)
    for load in loads:
        load.wait()

    def add(k):
        exchange(k, 1).wait_recv()
        far = sides(k)[1]
        onward[k] = (
            block(far, k)[...].astype(jnp.float32) + first[k, 1].astype(jnp.float32)
        ).astype(jnp.bfloat16)
        push(k).start()

    def close(k):
        exchange(k, 0).wait_recv()
        push(k).wait_recv()
        total = (
            block(place.dp, k)[...].astype(jnp.float32)
            + first[k, 0].astype(jnp.float32)
            + second[k].astype(jnp.float32)
        ).astype(jnp.bfloat16)
        mine[k] = total
        if k > 0:
            deliver(k).start()
        else:
            pltpu.make_async_copy(mine.at[0], returned.at[place.me], own_sem).start()

    lag = 2
    for n, k in enumerate(order):
        for done in range(n * pieces // owners, (n + 1) * pieces // owners):
            gradients(done)
        add(k)
        if n + ahead < owners:
            open_exchange(order[n + ahead])
        if n >= lag:
            close(order[n - lag])
    for k in order[owners - lag :]:
        close(k)
    for k in order:
        exchange(k, 0).wait_send()
        exchange(k, 1).wait_send()
        push(k).wait_send()
        if k > 0:
            deliver(k).wait()
    pltpu.make_async_copy(mine.at[0], returned.at[place.me], own_sem).wait()


def params(number):
    return pltpu.CompilerParams(
        collective_id=number, has_side_effects=True, vmem_limit_bytes=60 * 1024 * 1024
    )


ANY = pl.BlockSpec(memory_space=pl.ANY)
VMEM = pl.BlockSpec(memory_space=pltpu.VMEM)


def shards(sizes, queries, keys, values, resid, cotangent, zone_ids, norm_gain, w_in, w_out):
    rows = queries.shape[1]
    width = queries.shape[2]
    head_dim = width // HEADS
    groups, ring, pair = sizes
    owners = ring * pair
    heads = HEADS // ring
    capacity = 2 * rows // owners + 2
    padded = -(-capacity // 8) * 8
    dma = pltpu.SemaphoreType.DMA
    bf16, f32 = jnp.bfloat16, jnp.float32

    zone_of = zone_ids[0, :, 0]
    expert_hot = (zone_of[:, None] == jnp.arange(owners, dtype=jnp.int32)[None, :]).astype(
        jnp.int32
    )
    ranking = jnp.cumsum(expert_hot, axis=0) - 1
    slot_index = jnp.sum(ranking * expert_hot, axis=1)
    target = zone_of * padded + slot_index
    placing = (target[None, :] == jnp.arange(owners * padded, dtype=jnp.int32)[:, None]).astype(
        bf16
    )

    def placed(x):
        sent = jnp.dot(placing, x, preferred_element_type=f32).astype(bf16)
        return sent.reshape(owners, padded, width)

    slots = jax.ShapeDtypeStruct((groups * owners, padded, width), bf16)
    mixed, normed, arrived_g = pl.pallas_call(
        functools.partial(attend_kernel, sizes),
        out_shape=(
            jax.ShapeDtypeStruct((rows, width), f32),
            jax.ShapeDtypeStruct((rows, width), bf16),
            slots,
        ),
        in_specs=[ANY, ANY, ANY, VMEM, VMEM, VMEM],
        out_specs=(VMEM, VMEM, ANY),
        scratch_shapes=[
            pltpu.VMEM((3, heads, ring, rows, head_dim), bf16),
            pltpu.VMEM((heads, ring, rows, head_dim), bf16),
            pltpu.VMEM((ring, heads, rows, head_dim), bf16),
            dma((3, heads, ring - 1)),
            dma((3, heads, ring - 1)),
            dma((3, heads)),
            dma((heads, ring - 1)),
            dma((heads, ring - 1)),
            *dispatch_sems(owners),
        ],
        compiler_params=params(0),
        name="attend",
    )(queries[0], keys[0], values[0], resid[0], norm_gain[None, :], placed(cotangent[0]))

    slot_count = groups * owners * padded
    grads_in = arrived_g.reshape(slot_count, width)
    w_first = w_in[0]
    w_second = w_out[0]
    units = w_first.shape[1]
    inputs, hidden, d_pre = pl.pallas_call(
        functools.partial(dispatch_kernel, sizes),
        out_shape=(
            jax.ShapeDtypeStruct((slot_count, width), bf16),
            jax.ShapeDtypeStruct((slot_count, units), bf16),
            jax.ShapeDtypeStruct((slot_count, units), bf16),
        ),
        in_specs=[VMEM, ANY, ANY, ANY],
        out_specs=(VMEM, VMEM, VMEM),
        scratch_shapes=[
            pltpu.VMEM((slot_count, width), bf16),
            pltpu.VMEM(w_first.shape, bf16),
            pltpu.VMEM(w_second.shape, bf16),
            pltpu.VMEM((slot_count, units), f32),
            dma,
            dma,
            dma,
            *dispatch_sems(owners),
        ],
        compiler_params=params(1),
        name="dispatch",
    )(placed(normed), grads_in, w_first, w_second)

    part = jnp.dot(hidden, w_second, preferred_element_type=f32).astype(bf16)

    returned, grad_first, grad_second = pl.pallas_call(
        functools.partial(combine_kernel, sizes),
        out_shape=(
            jax.ShapeDtypeStruct((owners, padded, width), bf16),
            jax.ShapeDtypeStruct(w_first.shape, bf16),
            jax.ShapeDtypeStruct(w_second.shape, bf16),
        ),
        in_specs=[VMEM, ANY, ANY, ANY, ANY],
        out_specs=(VMEM, VMEM, VMEM),
        scratch_shapes=[
            pltpu.VMEM((owners, 2, padded, width), bf16),
            pltpu.VMEM((owners, padded, width), bf16),
            pltpu.VMEM((owners, padded, width), bf16),
            pltpu.VMEM((owners, padded, width), bf16),
            pltpu.VMEM((slot_count, width), bf16),
            pltpu.VMEM((slot_count, units), bf16),
            pltpu.VMEM((slot_count, units), bf16),
            pltpu.VMEM((slot_count, width), bf16),
            dma((owners, 2)),
            dma((owners, 2)),
            dma((owners,)),
            dma((owners,)),
            dma((owners,)),
            dma((owners,)),
            dma((4,)),
            dma,
        ],
        compiler_params=params(2),
        name="combine",
    )(part.reshape(groups * owners, padded, width), inputs, d_pre, hidden, grads_in)

    expert_rows = lax.dot_general(
        placing,
        returned.reshape(owners * padded, width),
        (((0,), (0,)), ((), ())),
        preferred_element_type=f32,
    )
    layer_out = (mixed + expert_rows).astype(bf16)[None]
    return (layer_out, grad_first[None], grad_second[None])


def solution(mesh):
    sizes = tuple(mesh.shape[name] for name in ("dp", "seq", "expert"))
    placed = (
        P(("dp", "expert"), "seq", None),
        P(("dp", "expert"), "seq", None),
        P(("dp", "expert"), "seq", None),
        P(("dp", "expert"), "seq", None),
        P(("dp", "expert"), "seq", None),
        P(("dp", "expert"), "seq", None),
        P(),
        P(("seq", "expert"), None, "dp"),
        P(("seq", "expert"), "dp", None),
    )
    return jax.shard_map(
        functools.partial(shards, sizes),
        mesh=mesh,
        in_specs=placed,
        out_specs=(
            P(("dp", "expert"), "seq", None),
            P(("seq", "expert"), None, "dp"),
            P(("seq", "expert"), "dp", None),
        ),
        check_vma=False,
    )
```
